32 devices in a mesh: enc: 4 (over z), ctx: 8 (over y, x, core).
Axes of the slice: x: 2, y: 2, z: 4, core: 2. Of those that a mesh axis runs over, the one named last changes fastest.
Arguments:
- patches: bfloat16 [3072, 1280], P('enc'), may hold values from -17 to 17
- patch_image: int32 [3072], P('enc'), may hold values from 63 to 767, as said below
- vit_gain: float32 [1280], replicated, may hold values from 0.1 to 1.9
- vit_qkv: bfloat16 [1280, 16, 240], P(None, 'ctx')
- vit_proj: bfloat16 [1280, 1280], P('ctx'), may hold values from -0.15625 to 0.15625
- merge_gain: float32 [1280], replicated, may hold values from 0.1 to 1.9
- merge_up: bfloat16 [5120, 5120], P(None, 'ctx'), may hold values from -0.078125 to 0.078125
- merge_down: bfloat16 [5120, 8192], P('ctx', 'enc'), may hold values from -0.078125 to 0.078125
- text_embed: bfloat16 [3072, 8192], P('ctx', 'enc'), may hold values from -17 to 17
- placeholder_unit: int32 [3072], replicated, may hold values from -1 to 767, as said below
- doc_id: int32 [3072], replicated, may hold values from 0 to 15, never falling along the last dimension, each value on 1 to 1920 neighbouring positions
- dec_gain: float32 [8192], replicated, may hold values from 0.1 to 1.9
- dec_wq: bfloat16 [8192, 2048], P(None, 'enc')
- dec_wk: bfloat16 [8192, 512], P(None, 'enc')
- dec_wv: bfloat16 [8192, 512], P(None, 'enc'), may hold values from -0.0625 to 0.0625
Outputs:
- attended: bfloat16 [3072, 2048], P('ctx', 'enc')
The draws below stay inside these ranges and needn't reach their ends.
Inputs may be any that keep to these rules, and one draw needn't show every extreme that they name: `patch_image`: the patches of an image are consecutive, start at a multiple of 4, number a multiple of 4 and at most 256, and lie within one aligned block of 768 patches; image numbers never fall and differ between images; in every such block some image has exactly 256 patches. `placeholder_unit`: -1 marks a text position. Every unit appears exactly once; the units of one image fill consecutive placeholders in their order; the placeholders of an aligned block of 384 positions are consecutive and number at most 192, and some block holds exactly 192. `doc_id`: document numbers never fall; a document has at most 1920 positions, and some document exactly 1920.
All inputs are finite; a program needn't handle non-finite values.
Results may differ from the reference program's by a relative error of at most 0.0085.
Values may be sent and summed in bfloat16 or wider, within the bound.
No kernel may reach another device: no remote copies, remote signals or barrier semaphores. Data moves between devices by JAX's collectives and lax.ppermute only.
A program may use at most 128 MiB of HBM per device.

```python
import math
import jax
import jax.numpy as jnp
import numpy as np
from jax import lax

VW = 1280
VH = 16
D = 8192
HD = 128
QPK = 4
IMG_MAX = 256
TOK_CTX = 384
VHD = 80
MW = 5120
KV_HEADS = 4
TOKENS = 3072
PATCHES = 3072
GROUP_PATCHES = 768
UNITS = 768
DOCS = 16
DOC_MAX = 1920
N_ENC = 4
N_CTX = 8


def drawn_table(key, row_count, col_count):
    return jnp.clip(jax.random.normal(jax.random.fold_in(key, 1), (row_count, col_count), jnp.float32), -4.0, 4.0)


def draw_patches(key, part):
    values = drawn_table(jax.random.fold_in(key, 101), PATCHES, VW)
    return values.astype(jnp.bfloat16)


def draw_text_embed(key, part):
    values = drawn_table(jax.random.fold_in(key, 102), TOKENS, D)
    return values.astype(jnp.bfloat16)


def unit_images(key):
    group_units = PATCHES // (4 * N_ENC)
    most_units = IMG_MAX // 4
    chance = jax.random.randint(jax.random.fold_in(key, 11), (N_ENC, group_units), 0, max(most_units // 2, 1))
    places = jnp.arange(group_units, dtype=jnp.int32)
    cuts = (chance == 0) | (places % most_units == 0)[None, :]
    cuts = jnp.where((places < most_units)[None, :], (places == 0)[None, :], cuts)
    closing = jnp.concatenate([cuts[:, 1:], jnp.ones((N_ENC, 1), dtype=bool)], axis=1)
    marks = jnp.where(closing, places[None, :], group_units).astype(jnp.int32)
    last_unit = lax.cummin(marks, axis=1, reverse=True)
    return (last_unit + group_units * jnp.arange(N_ENC, dtype=jnp.int32)[:, None]).reshape(-1).astype(jnp.int32)


def draw_patch_image(key, part):
    return jnp.repeat(unit_images(key), 4).astype(jnp.int32)


def draw_placeholder_unit(key, part):
    images = unit_images(key)
    image_rank = jax.random.permutation(jax.random.fold_in(key, 12), UNITS).astype(jnp.int32)
    scores = image_rank[images] * UNITS + jnp.arange(UNITS, dtype=jnp.int32)
    unit_order = jnp.argsort(scores, stable=True).astype(jnp.int32)
    quarter = TOK_CTX // 4
    pair_count = N_CTX // 2
    shifts = jax.random.randint(jax.random.fold_in(key, 13), (pair_count,), -quarter, quarter + 1)
    chosen = jax.random.randint(jax.random.fold_in(key, 14), (), 0, pair_count)
    flip_sign = 2 * jax.random.randint(jax.random.fold_in(key, 15), (), 0, 2) - 1
    shifts = jnp.where(jnp.arange(pair_count) == chosen, flip_sign * quarter, shifts)
    counts = jnp.stack([quarter + shifts, quarter - shifts], axis=1).reshape(-1)
    counts = counts[jax.random.permutation(jax.random.fold_in(key, 16), N_CTX)]
    starts = jax.random.randint(jax.random.fold_in(key, 17), (N_CTX,), 0, TOK_CTX - counts + 1)
    before = jnp.cumsum(counts) - counts
    places = jnp.arange(TOK_CTX, dtype=jnp.int32)
    inside = (places[None, :] >= starts[:, None]) & (places[None, :] < (starts + counts)[:, None])
    global_rank = jnp.clip(before[:, None] + places[None, :] - starts[:, None], 0, UNITS - 1)
    return jnp.where(inside, unit_order[global_rank], -1).reshape(-1).astype(jnp.int32)


def draw_vit_qkv(key, part):
    base = jnp.clip(jax.random.normal(jax.random.fold_in(key, 41), (VW, VH, 3, VHD), jnp.float32), -4.0, 4.0) * VW ** (-0.5)
    return base.reshape(VW, VH, 3 * VHD).astype(jnp.bfloat16)


def key_table(key):
    return jnp.clip(jax.random.normal(jax.random.fold_in(key, 31), (D, KV_HEADS, HD), jnp.float32), -4.0, 4.0) * D ** (-0.5)


def draw_dec_wk(key, part):
    return key_table(key).reshape(D, KV_HEADS * HD).astype(jnp.bfloat16)


def draw_dec_wq(key, part):
    noise = jnp.clip(jax.random.normal(jax.random.fold_in(key, 32), (D, KV_HEADS, QPK, HD), jnp.float32), -4.0, 4.0) * D ** (-0.5)
    return noise.reshape(D, KV_HEADS * QPK * HD).astype(jnp.bfloat16)


def steps_of(rng, extent, split, low, top_value):
    gain, own = 1.0, jax.random.fold_in(rng, 6)
    for dim, shards_of in split:
        draws = jnp.exp(jax.random.uniform(jax.random.fold_in(own, dim), (shards_of,), jnp.float32, low / len(split), top_value / len(split)))
        gain = gain * jnp.repeat(draws, extent[dim] // shards_of).reshape([-1 if axis == dim else 1 for axis in range(len(extent))])
    return gain


def split_up(amount, total, bound, skew):
    loads = [(1 << 20) // math.isqrt(grade ** skew) + 1 for grade in range(2, amount + 1)]
    rest, given = total - bound - (amount - 1), [1] * (amount - 1)
    while rest > 0:
        movable = [i for i in range(amount - 1) if given[i] < bound]
        whole, left = sum([loads[i] for i in movable]), rest
        for i in movable:
            addition = min(bound - given[i], max(1, left * loads[i] // whole), rest)
            given[i] = given[i] + addition
            rest = rest - addition
    return np.array([bound] + given)


def ragged_sizes(stream_key, number_of, total, limit, lean):
    if number_of == 2:
        one = jax.random.randint(stream_key, (), max(1, total - limit), min(limit, total - 1) + 1)
        return jnp.stack([one, total - one])
    tallies = jnp.asarray(split_up(number_of, total, limit, lean), jnp.int32)
    couples = (number_of - 1) // 2
    source_of, receiver = tallies[1:1 + 2 * couples:2], tallies[2:2 + 2 * couples:2]
    slack = jnp.minimum(source_of - 1, limit - receiver)
    passed = jax.random.randint(jax.random.fold_in(stream_key, 1), (couples,), 0, 1 << 20) % (slack + 1)
    tallies = tallies.at[1:1 + 2 * couples:2].set(source_of - passed).at[2:2 + 2 * couples:2].set(receiver + passed)
    return tallies[jax.random.permutation(jax.random.fold_in(stream_key, 2), number_of)]


def normal_values(stream_key, shape, deviation, limit, split=(), held_as=jnp.bfloat16):
    loudness = steps_of(stream_key, shape, split, -0.22, 0.18) if split else 1.0
    drawn = jax.random.normal(stream_key, shape, jnp.float32) * deviation * loudness
    return jnp.minimum(jnp.maximum(drawn, -limit), limit).astype(held_as)


def setup_inputs(seed: int = 0) -> dict:
    streams_of = jax.random.split(jax.random.key(seed), 16)
    return {
        "patches": draw_patches(jax.random.fold_in(streams_of[15], 71), 0),
        "patch_image": draw_patch_image(jax.random.fold_in(streams_of[15], 71), 0),
        "vit_gain": jnp.clip(1.0 + 0.18 * jax.random.normal(streams_of[2], (VW,), jnp.float32), 0.1, 1.9),
        "vit_qkv": draw_vit_qkv(jax.random.fold_in(streams_of[15], 71), 0),
        "vit_proj": normal_values(streams_of[4], (VH * VHD, VW), VW ** -0.5, 0.15625, ((0, 8),)),
        "merge_gain": jnp.clip(1.0 + 0.18 * jax.random.normal(streams_of[5], (VW,), jnp.float32), 0.1, 1.9),
        "merge_up": normal_values(streams_of[6], (MW, MW), MW ** -0.5, 0.078125, ((1, 8),)),
        "merge_down": normal_values(streams_of[7], (MW, D), MW ** -0.5, 0.078125, ((0, 8), (1, 4))),
        "text_embed": draw_text_embed(jax.random.fold_in(streams_of[15], 71), 0),
        "placeholder_unit": draw_placeholder_unit(jax.random.fold_in(streams_of[15], 71), 0),
        "doc_id": jnp.searchsorted(jnp.cumsum(ragged_sizes(streams_of[10], DOCS, TOKENS, DOC_MAX, 2)), jnp.arange(TOKENS), side="right").astype(jnp.int32),
        "dec_gain": jnp.clip(1.0 + 0.18 * jax.random.normal(streams_of[11], (D,), jnp.float32), 0.1, 1.9),
        "dec_wq": draw_dec_wq(jax.random.fold_in(streams_of[15], 71), 0),
        "dec_wk": draw_dec_wk(jax.random.fold_in(streams_of[15], 71), 0),
        "dec_wv": normal_values(streams_of[14], (D, KV_HEADS * HD), D ** -0.5, 0.0625, ((1, 4),)),
    }


EPSILON = 1e-06
NEGATIVE = -1e+30

def layer_norm(values, scaling):
    widened = values.astype(jnp.float32)
    center = widened - lax.optimization_barrier(jnp.mean(widened, axis=1, keepdims=True))
    spread = lax.optimization_barrier(jnp.mean(center * center, axis=1, keepdims=True))
    return (center * lax.rsqrt(spread + EPSILON) * scaling).astype(jnp.bfloat16)

def masked_attention(queries, keys_in, values_in, allowed_rows):
    head_count, row_count, head_width = queries.shape
    block_rows = math.gcd(row_count, 512)
    scaling = head_width ** (-0.5)
    keys_wide = keys_in.astype(jnp.float32)
    values_wide = values_in.astype(jnp.float32)

    def one_block(offset):
        query_block = lax.dynamic_slice_in_dim(queries, offset, block_rows, 1).astype(jnp.float32)
        allowed = allowed_rows(offset, block_rows)
        scores = jnp.einsum('hqd,hkd->hqk', query_block, keys_wide) * scaling
        scores = jnp.where(allowed[None], scores, NEGATIVE)
        highest = lax.optimization_barrier(jnp.max(scores, axis=2, keepdims=True))
        weights = jnp.exp(scores - highest)
        totals = lax.optimization_barrier(jnp.sum(weights, axis=2, keepdims=True))
        rounded = lax.optimization_barrier(weights.astype(jnp.bfloat16)).astype(jnp.float32)
        mixture = jnp.einsum('hqk,hkd->hqd', rounded, values_wide)
        return (mixture / totals).astype(jnp.bfloat16)
    offsets = (jnp.arange(row_count // block_rows) * block_rows).astype(jnp.int32)
    blocks = lax.map(one_block, offsets)
    return blocks.transpose(1, 0, 2, 3).reshape(head_count, row_count, head_width)

def reference(patches, patch_image, vit_gain, vit_qkv, vit_proj, merge_gain, merge_up, merge_down, text_embed, placeholder_unit, doc_id, dec_gain, dec_wq, dec_wk, dec_wv):

    def vision_group(inputs):
        group_rows, group_ids = inputs
        normed = layer_norm(group_rows, vit_gain)
        packed = jnp.dot(normed, vit_qkv.reshape(VW, VH * 3 * VHD), preferred_element_type=jnp.float32)
        packed = packed.astype(jnp.bfloat16).reshape(GROUP_PATCHES, VH, 3, VHD).transpose(2, 1, 0, 3)

        def same_image(offset, block_rows):
            block_ids = lax.dynamic_slice_in_dim(group_ids, offset, block_rows, 0)
            return block_ids[:, None] == group_ids[None, :]
        attended_heads = masked_attention(packed[0], packed[1], packed[2], same_image)
        flat_heads = attended_heads.transpose(1, 0, 2).reshape(GROUP_PATCHES, VH * VHD)
        head_terms = jnp.dot(flat_heads, vit_proj, preferred_element_type=jnp.float32)
        vit_out = (group_rows.astype(jnp.float32) + head_terms).astype(jnp.bfloat16)
        return layer_norm(lax.optimization_barrier(vit_out), merge_gain)
    merged = lax.map(vision_group, (patches.reshape(N_ENC, GROUP_PATCHES, VW), patch_image.reshape(N_ENC, GROUP_PATCHES)))
    unit_inputs = merged.reshape(UNITS, 4 * VW)
    hidden = jax.nn.gelu(jnp.dot(unit_inputs, merge_up, preferred_element_type=jnp.float32), approximate=False).astype(jnp.bfloat16)
    vision_rows = jnp.dot(hidden, merge_down, preferred_element_type=jnp.float32).astype(jnp.bfloat16)
    unit_index = jnp.clip(placeholder_unit, 0, UNITS - 1).astype(jnp.int32)
    sequence = jnp.where((placeholder_unit >= 0)[:, None], jnp.take(vision_rows, unit_index, axis=0), text_embed)
    widened = sequence.astype(jnp.float32)
    normed = (widened * lax.rsqrt(lax.optimization_barrier(jnp.mean(widened * widened, axis=1, keepdims=True)) + EPSILON) * dec_gain).astype(jnp.bfloat16)
    queries = jnp.dot(normed, dec_wq, preferred_element_type=jnp.float32).astype(jnp.bfloat16)
    queries = queries.reshape(TOKENS, KV_HEADS, QPK, HD).transpose(1, 2, 0, 3)
    keys_all = jnp.dot(normed, dec_wk, preferred_element_type=jnp.float32).astype(jnp.bfloat16)
    keys_all = keys_all.reshape(TOKENS, KV_HEADS, HD).transpose(1, 0, 2)
    values_all = jnp.dot(normed, dec_wv, preferred_element_type=jnp.float32).astype(jnp.bfloat16)
    values_all = values_all.reshape(TOKENS, KV_HEADS, HD).transpose(1, 0, 2)
    positions = jnp.arange(TOKENS, dtype=jnp.int32)

    def causal_docs(offset, block_rows):
        query_pos = offset + jnp.arange(block_rows, dtype=jnp.int32)
        query_docs = lax.dynamic_slice_in_dim(doc_id, offset, block_rows, 0)
        return (positions[None, :] <= query_pos[:, None]) & (doc_id[None, :] == query_docs[:, None])

    def one_group(inputs):
        group_queries, group_keys, group_values = inputs
        shared_keys = jnp.broadcast_to(group_keys[None], (QPK, TOKENS, HD))
        shared_values = jnp.broadcast_to(group_values[None], (QPK, TOKENS, HD))
        return masked_attention(group_queries, shared_keys, shared_values, causal_docs)
    attended = lax.map(one_group, (queries, keys_all, values_all))
    return attended.transpose(2, 0, 1, 3).reshape(TOKENS, KV_HEADS * QPK * HD)
```

```python
import functools
import math

import jax
import jax.numpy as jnp
from jax import lax
from jax.experimental import pallas as pl
from jax.experimental.pallas import tpu as pltpu
from jax.sharding import PartitionSpec as P

HD = 128
QPK = 4
EPSILON = 1e-06
NEGATIVE = -1e30
F32 = jnp.float32
BF16 = jnp.bfloat16


VMEM_SPEC = pl.BlockSpec(memory_space=pltpu.VMEM)
SMEM_SPEC = pl.BlockSpec(memory_space=pltpu.SMEM)
ANY_SPEC = pl.BlockSpec(memory_space=pl.ANY)
NT = (((1,), (1,)), ((), ()))
TN = (((0,), (0,)), ((), ()))


def dot(a, b, dims=(((1,), (0,)), ((), ()))):
    return lax.dot_general(a, b, dims, preferred_element_type=F32)


def rows_norm(values, scaling):
    center = values - jnp.mean(values, axis=1, keepdims=True)
    spread = jnp.mean(center * center, axis=1, keepdims=True)
    return center * lax.rsqrt(spread + EPSILON) * scaling


def image_kernel(heads, width, x_ref, gain_ref, w_ref, row_ref, col_ref, o_ref):
    rows = x_ref.shape[0]
    normed = rows_norm(x_ref[...].astype(F32), gain_ref[...]).astype(BF16)
    scaling = width ** (-0.5)
    step = math.gcd(rows, 256)
    for h in range(heads):
        base = h * 3 * width
        q_t = dot(w_ref[base : base + width, :], normed, NT).astype(BF16)
        k_n = dot(normed, w_ref[base + width : base + 2 * width, :], NT).astype(BF16)
        v_t = dot(w_ref[base + 2 * width : base + 3 * width, :], normed, NT).astype(BF16)
        for begin in range(0, rows, step):
            same = col_ref[...] == row_ref[:, begin : begin + step]
            scores = dot(k_n, q_t[:, begin : begin + step]) * scaling
            scores = jnp.where(same, scores, NEGATIVE)
            weights = jnp.exp(scores - jnp.max(scores, axis=0, keepdims=True))
            totals = jnp.sum(weights, axis=0, keepdims=True)
            mixed = dot(v_t, weights.astype(BF16)) / totals
            o_ref[h * width : (h + 1) * width, begin : begin + step] = mixed.astype(BF16)


def image_attention(patches, gain, w_t, ids, heads, width):
    rows = patches.shape[0]
    return pl.pallas_call(
        functools.partial(image_kernel, heads, width),
        out_shape=jax.ShapeDtypeStruct((heads * width, rows), BF16),
        in_specs=[VMEM_SPEC] * 5,
        out_specs=VMEM_SPEC,
        name="image_attention",
    )(patches, gain[None, :], w_t, ids[None, :], ids[:, None])


def merge_kernel(parts, x_ref, gain_ref, up_hbm, *refs):
    heads, projs = refs[:parts], refs[parts : 2 * parts]
    o_ref, up_ref, rows_ref, sems = refs[2 * parts :]
    rows, wide = x_ref.shape
    units = rows // 4
    copies = [
        pltpu.make_async_copy(
            up_hbm.at[pl.ds(j * wide, wide), :], up_ref.at[pl.ds(j * wide, wide), :], sems.at[j]
        )
        for j in range(4)
    ]
    for copy in copies:
        copy.start()
    total = x_ref[...].astype(F32)
    for a_ref, p_ref in zip(heads, projs):
        total = total + dot(a_ref[...], p_ref[...], TN)
    out = total.astype(BF16).astype(F32)
    normed = rows_norm(out, gain_ref[...])
    lanes = rows_ref.shape[2]
    for i in range(wide // lanes):
        rows_ref[i] = normed[:, i * lanes : (i + 1) * lanes]
    hidden = jnp.zeros((units, o_ref.shape[1]), F32)
    for j in range(4):
        copies[j].wait()
        fourth = [rows_ref[i, pl.ds(j, units, stride=4), :] for i in range(wide // lanes)]
        hidden = hidden + dot(
            jnp.concatenate(fourth, axis=1).astype(BF16), up_ref[j * wide : (j + 1) * wide, :]
        )
    o_ref[...] = (0.5 * hidden * (1.0 + lax.erf(hidden * (2.0 ** -0.5)))).astype(BF16)


def merge_up_product(patches, gain, merge_up, heads, projs):
    rows, wide = patches.shape
    columns = merge_up.shape[1]
    return pl.pallas_call(
        functools.partial(merge_kernel, len(heads)),
        out_shape=jax.ShapeDtypeStruct((rows // 4, columns), BF16),
        in_specs=[VMEM_SPEC, VMEM_SPEC, ANY_SPEC] + [VMEM_SPEC] * (2 * len(heads)),
        out_specs=VMEM_SPEC,
        scratch_shapes=[
            pltpu.VMEM((4 * wide, columns), BF16),
            pltpu.VMEM((wide // 128, rows, 128), F32),
            pltpu.SemaphoreType.DMA((4,)),
        ],
        name="merge_up",
    )(patches, gain[None, :], merge_up, *heads, *projs)


def source_of(block, place, own, below, above):
    if block == place:
        return own
    return below[place - block - 1] if block < place else above[block - place - 1]


def line_gather(values, axis, size):
    below, above = [], []
    up = down = values
    for k in range(1, size):
        up = lax.ppermute(up, axis, [(i, i + 1) for i in range(k - 1, size - 1)])
        down = lax.ppermute(down, axis, [(i + 1, i) for i in range(0, size - k)])
        below.append(up)
        above.append(down)
    return below, above


def down_kernel(size, count, place_ref, down_ref, *refs):
    own, below, above = refs[0], refs[1:size], refs[size : 2 * size - 1]
    keep_ref, send_ref, hidden_ref = refs[2 * size - 1 :]
    rows = own.shape[0]
    unit_rows = rows * size // count
    place, index = place_ref[0], place_ref[1]
    for z in range(size):

        @pl.when(place == z)
        def _():
            for block in range(size):
                source = source_of(block, z, own, below, above)
                for part in range(rows // unit_rows):
                    target = (block * rows // unit_rows + part) ^ index
                    slot = (target >> 1) + (target & 1) * (count // 2)
                    hidden_ref[pl.ds(pl.multiple_of(slot * unit_rows, 16), unit_rows), :] = source[
                        part * unit_rows : (part + 1) * unit_rows, :
                    ]

    half = rows * size // 2
    send_ref[...] = dot(hidden_ref[half:, :], down_ref[...]).astype(BF16)
    keep_ref[...] = dot(hidden_ref[:half, :], down_ref[...]).astype(BF16)


def merge_down_product(place, merge_down, own, below, above, count):
    size = len(below) + 1
    rows = own.shape[0] * size
    shape = jax.ShapeDtypeStruct((rows // 2, merge_down.shape[1]), BF16)
    return pl.pallas_call(
        functools.partial(down_kernel, size, count),
        out_shape=(shape, shape),
        in_specs=[SMEM_SPEC] + [VMEM_SPEC] * (2 * size),
        out_specs=(VMEM_SPEC, VMEM_SPEC),
        scratch_shapes=[pltpu.VMEM((rows, own.shape[1]), BF16)],
        name="merge_down",
    )(place, merge_down, own, *below, *above)


def project_kernel(size, place_ref, gain_ref, wq_ref, wk_ref, wv_ref, *refs):
    own, below, above = refs[0], refs[1:size], refs[size : 2 * size - 1]
    o_ref, rows_ref, total_ref, square_ref, sems = refs[2 * size - 1 :]
    step = pl.program_id(0)
    q_cols, k_cols = wq_ref.shape[1], wk_ref.shape[1]

    @pl.when(step == 0)
    def _():
        for z in range(size):

            @pl.when(place_ref[0] == z)
            def _():
                for block in range(size):
                    pltpu.make_async_copy(
                        source_of(block, z, own, below, above), rows_ref.at[block], sems.at[block]
                    ).start()

    pltpu.make_async_copy(own, rows_ref.at[step], sems.at[step]).wait()
    wide = rows_ref[step].astype(F32)
    squares = jnp.sum(wide * wide, axis=1, keepdims=True)
    scaled = (wide * gain_ref[0]).astype(BF16)
    parts = [dot(scaled, w_ref[...]) for w_ref in (wq_ref, wk_ref, wv_ref)]
    bounds = (0, q_cols, q_cols + k_cols, total_ref.shape[1])

    @pl.when(step == 0)
    def _():
        square_ref[...] = squares
        for i, part in enumerate(parts):
            total_ref[:, bounds[i] : bounds[i + 1]] = part

    @pl.when(step > 0)
    def _():
        square_ref[...] += squares
        for i, part in enumerate(parts):
            total_ref[:, bounds[i] : bounds[i + 1]] += part

    @pl.when(step == size - 1)
    def _():
        features = size * own.shape[1]
        scale = lax.rsqrt(square_ref[...] / features + EPSILON)
        o_ref[...] = (total_ref[...] * scale).astype(BF16)


def project(place, gain, wq, wk, wv, own, below, above, name):
    size = len(below) + 1
    rows, part = own.shape
    columns = wq.shape[1] + wk.shape[1] + wv.shape[1]
    weight = lambda w: pl.BlockSpec((part, w.shape[1]), lambda k: (k, 0))
    return pl.pallas_call(
        functools.partial(project_kernel, size),
        out_shape=jax.ShapeDtypeStruct((rows, columns), BF16),
        grid=(size,),
        in_specs=[SMEM_SPEC, pl.BlockSpec((1, 1, part), lambda k: (k, 0, 0))]
        + [weight(w) for w in (wq, wk, wv)]
        + [ANY_SPEC] * (2 * size - 1),
        out_specs=pl.BlockSpec((rows, columns), lambda k: (0, 0)),
        scratch_shapes=[
            pltpu.VMEM((size, rows, part), BF16),
            pltpu.VMEM((rows, columns), F32),
            pltpu.VMEM((rows, 1), F32),
            pltpu.SemaphoreType.DMA((size,)),
        ],
        compiler_params=pltpu.CompilerParams(dimension_semantics=("arbitrary",)),
        name=name,
    )(place, gain.reshape(size, 1, part), wq, wk, wv, own, *below, *above)


def attend_kernel(count, place_ref, first_ref, last_ref, docs_ref, doc_ref, slot_ref, text_ref, *refs):
    keys, pool = refs[:count], refs[count : 2 * count]
    o_ref, pool_ref, query_ref, top_ref, sum_ref, mix_ref = refs[2 * count :]
    rows = text_ref.shape[0]
    units = pool[0].shape[0]
    index = place_ref[1]
    scaling = HD ** (-0.5)
    for m in range(count):
        pool_ref[m * units : (m + 1) * units, :] = pool[m][...]
    pool_rows = count * units
    q_cols = QPK * HD

    def picked(block, low, high, text):
        slots = slot_ref[pl.ds(pl.multiple_of(block * rows, 128), rows), :]
        chosen = slots == lax.broadcasted_iota(jnp.int32, (rows, pool_rows), 1)
        vision = dot(chosen.astype(F32).astype(BF16), pool_ref[:, low:high])
        return jnp.where(slots >= 0, vision, text.astype(F32)).astype(BF16)

    query_ref[...] = picked(index, 0, q_cols, text_ref[...])
    top_ref[...] = jnp.full(top_ref.shape, NEGATIVE, F32)
    sum_ref[...] = jnp.zeros(sum_ref.shape, F32)
    mix_ref[...] = jnp.zeros(mix_ref.shape, F32)
    query_docs = doc_ref[...]
    query_pos = index * rows + lax.broadcasted_iota(jnp.int32, (rows, rows), 0)
    for m in range(count):
        block = index ^ m
        visible = (block <= index) & (last_ref[block] >= first_ref[index])

        @pl.when(visible)
        def _():
            both = picked(block, q_cols, q_cols + 2 * HD, keys[m][...])
            key_pos = block * rows + lax.broadcasted_iota(jnp.int32, (rows, rows), 1)
            allowed = (query_docs == docs_ref[block]) & (key_pos <= query_pos)
            for j in range(QPK):
                scores = dot(query_ref[:, j * HD : (j + 1) * HD], both[:, :HD], NT) * scaling
                scores = jnp.where(allowed, scores, NEGATIVE)
                old = top_ref[j]
                peak = jnp.maximum(old, jnp.max(scores, axis=1, keepdims=True))
                factor = jnp.exp(old - peak)
                weights = jnp.exp(scores - peak)
                top_ref[j] = peak
                sum_ref[j] = sum_ref[j] * factor + jnp.sum(weights, axis=1, keepdims=True)
                mix_ref[j] = mix_ref[j] * factor + dot(weights.astype(BF16), both[:, HD:])

    for j in range(QPK):
        o_ref[:, j * HD : (j + 1) * HD] = (mix_ref[j] / sum_ref[j]).astype(BF16)


def attend(place, first, last, docs, doc_own, slots, text_q, keys, pool):
    count = len(keys)
    rows = text_q.shape[0]
    units, columns = pool[0].shape
    return pl.pallas_call(
        functools.partial(attend_kernel, count),
        out_shape=jax.ShapeDtypeStruct((rows, QPK * HD), BF16),
        in_specs=[SMEM_SPEC] * 3 + [VMEM_SPEC] * (4 + 2 * count),
        out_specs=VMEM_SPEC,
        scratch_shapes=[
            pltpu.VMEM((count * units, columns), BF16),
            pltpu.VMEM((rows, QPK * HD), BF16),
            pltpu.VMEM((QPK, rows, 1), F32),
            pltpu.VMEM((QPK, rows, 1), F32),
            pltpu.VMEM((QPK, rows, HD), F32),
        ],
        name="attend",
    )(place, first, last, docs, doc_own, slots, text_q, *keys, *pool)


def xor_gather(values, axis, size):
    pairs = lambda m: [(i, i ^ m) for i in range(size)]
    slots = [values] + [None] * (size - 1)
    for m in range(2, size, 2):
        slots[m] = lax.ppermute(values, axis, pairs(m))
    for m in range(0, size, 2):
        slots[m + 1] = lax.ppermute(slots[m], axis, pairs(1))
    return slots


def body(
    size,
    count,
    patches,
    patch_image,
    vit_gain,
    vit_qkv,
    vit_proj,
    merge_gain,
    merge_up,
    merge_down,
    text_embed,
    placeholder_unit,
    doc_id,
    dec_gain,
    dec_wq,
    dec_wk,
    dec_wv,
):
    enc_index = lax.axis_index("enc")
    ctx_index = lax.axis_index("ctx")
    place = jnp.stack([enc_index, ctx_index]).astype(jnp.int32)
    heads, width = vit_qkv.shape[1], vit_qkv.shape[2] // 3
    tok_rows = text_embed.shape[0]

    text_below, text_above = line_gather(text_embed, "enc", size)
    projs = xor_gather(vit_proj, "ctx", count)

    w_t = vit_qkv.transpose(1, 2, 0).reshape(heads * 3 * width, vit_qkv.shape[0])
    mixed = image_attention(patches, vit_gain, w_t, patch_image, heads, width)
    mixed_slots = xor_gather(mixed, "ctx", count)
    hidden = merge_up_product(patches, merge_gain, merge_up, mixed_slots, projs)
    below, above = line_gather(hidden, "enc", size)
    keep, send = merge_down_product(place, merge_down, hidden, below, above, count)
    pairs = lambda m: [(i, i ^ m) for i in range(count)]
    other = lax.ppermute(send, "ctx", pairs(1))
    units = keep.shape[0] // (count // 2)
    added = keep.astype(F32) + other.astype(F32)
    vision = added[:units]
    for i in range(1, count // 2):
        rows = added[i * units : (i + 1) * units].astype(BF16)
        vision = vision + lax.ppermute(rows, "ctx", pairs(2 * i)).astype(F32)
    vision = vision.astype(BF16)
    below, above = line_gather(vision, "enc", size)

    text_out = project(
        place, dec_gain, dec_wq, dec_wk, dec_wv, text_embed, text_below, text_above, "project_text"
    )
    q_cols = dec_wq.shape[1]
    text_kv = xor_gather(text_out[:, q_cols:], "ctx", count)
    pool_own = project(
        place, dec_gain, dec_wq, dec_wk, dec_wv, vision, below, above, "project_vision"
    )
    pool = xor_gather(pool_own, "ctx", count)

    unit = placeholder_unit
    slots = jnp.where(unit >= 0, ((unit // units) ^ ctx_index) * units + unit % units, -1)
    docs = doc_id.reshape(count, 1, tok_rows)
    doc_own = lax.dynamic_slice_in_dim(doc_id, ctx_index * tok_rows, tok_rows, 0)
    return attend(
        place,
        docs[:, 0, 0],
        docs[:, 0, -1],
        docs,
        doc_own[:, None],
        slots[:, None].astype(jnp.int32),
        text_out[:, :q_cols],
        text_kv,
        pool,
    )


def solution(mesh):
    placed = (
        P("enc", None),
        P("enc"),
        P(),
        P(None, "ctx", None),
        P("ctx", None),
        P(),
        P(None, "ctx"),
        P("ctx", "enc"),
        P("ctx", "enc"),
        P(),
        P(),
        P(),
        P(None, "enc"),
        P(None, "enc"),
        P(None, "enc"),
    )
    return jax.shard_map(
        functools.partial(body, mesh.shape["enc"], mesh.shape["ctx"]),
        mesh=mesh,
        in_specs=placed,
        out_specs=P("ctx", "enc"),
        check_vma=False,
    )
```
